32 devices in a mesh: groups: 1, row: 32 (over z, y, x, core), col: 1.
Axes of the slice: x: 2, y: 2, z: 4, core: 2. Of those that a mesh axis runs over, the one named last changes fastest.
Arguments:
- features_in: bfloat16 [64, 128, 128], P(None, ('groups', 'row'), 'col'), may hold values from -6 to 6
- gain_outer: float32 [8, 64], replicated, may hold values from 0.25 to 1.75
- bias_outer: float32 [8, 64], replicated, may hold values from -3 to 3
- w_narrow: bfloat16 [8, 32, 576], replicated, may hold values from -0.25 to 0.25
- gain_inner: float32 [8, 32], replicated, may hold values from 0.25 to 1.75
- bias_inner: float32 [8, 32], replicated, may hold values from -3 to 3
- w_widen: bfloat16 [8, 64, 288], replicated, may hold values from -0.375 to 0.375
Outputs:
- features_out: bfloat16 [64, 128, 128], P(None, ('groups', 'row'), 'col')
The draws below stay inside these ranges and needn't reach their ends.
All inputs are finite; a program needn't handle non-finite values.
Results may differ from the reference program's by a relative error of at most 0.022.
Values may be sent and summed in bfloat16 or wider, within the bound.
No kernel may reach another device: no remote copies, remote signals or barrier semaphores. Data moves between devices by JAX's collectives and lax.ppermute only.
A program may use at most 64 MiB of HBM per device.

```python
import jax
import jax.numpy as jnp
from jax import lax

CH = 64
MID = 32
ROUNDS = 2
BLOCKS = 8
L = 128


def steps_of(stream_key, extent, shards, smallest, top_value):
    factor_of = 1.0
    for dim, parts in shards:
        heights = jax.random.uniform(jax.random.fold_in(jax.random.fold_in(stream_key, 6), dim), (parts,), jnp.float32, smallest / len(shards), top_value / len(shards))
        factor_of = factor_of * jnp.repeat(jnp.exp(heights), extent[dim] // parts).reshape((-1,) + (1,) * (len(extent) - 1 - dim))
    return factor_of


def noise(own_key, dims, scale, reach, split=(), held_as=jnp.bfloat16):
    factor_of = steps_of(own_key, dims, split, -0.22, 0.18) if split else 1.0
    array = jax.random.normal(own_key, dims, jnp.float32) * scale * factor_of
    return jnp.minimum(jnp.maximum(array, -reach), reach).astype(held_as)


def setup_inputs(seed: int = 0, part: int = 0) -> dict:
    arg_keys = jax.random.split(jax.random.key(seed), 8)
    own_keys = jax.random.split(jax.random.fold_in(arg_keys[7], part), 8)
    features_in = noise(own_keys[0], (CH, L, L), 1.0, 6.0, ((1, 32),))
    gain_outer = jnp.clip(1.0 + 0.15 * jax.random.normal(arg_keys[1], (BLOCKS, CH), jnp.float32), 0.25, 1.75)
    bias_outer = noise(arg_keys[2], (BLOCKS, CH), 0.5, 3.0, (), jnp.float32)
    w_narrow = noise(arg_keys[3], (BLOCKS, MID, 9 * CH), (9 * CH) ** -0.5, 0.25)
    gain_inner = jnp.clip(1.0 + 0.15 * jax.random.normal(arg_keys[4], (BLOCKS, MID), jnp.float32), 0.25, 1.75)
    bias_inner = noise(arg_keys[5], (BLOCKS, MID), 0.5, 3.0, (), jnp.float32)
    w_widen = noise(arg_keys[6], (BLOCKS, CH, 9 * MID), (9 * MID) ** -0.5, 0.375)
    return {"features_in": features_in, "gain_outer": gain_outer, "bias_outer": bias_outer, "w_narrow": w_narrow, "gain_inner": gain_inner, "bias_inner": bias_inner, "w_widen": w_widen}


def dilated_conv(hidden, weight, dilation):
    out_count = weight.shape[0]
    in_count = hidden.shape[0]
    kernel = weight.astype(jnp.float32).reshape(out_count, 3, 3, in_count).transpose(0, 3, 1, 2)
    result = lax.conv_general_dilated(hidden[None], kernel, (1, 1), ((dilation, dilation), (dilation, dilation)), rhs_dilation=(dilation, dilation), dimension_numbers=("NCHW", "OIHW", "NCHW"), precision=lax.Precision.HIGHEST)
    return result[0]


def reference(features_in, gain_outer, bias_outer, w_narrow, gain_inner, bias_inner, w_widen):
    stream = features_in
    for repeat in range(ROUNDS):
        stream_f = stream.astype(jnp.float32)
        stream = ((stream_f + jnp.transpose(stream_f, (0, 2, 1))) * 0.5).astype(jnp.bfloat16)
        for within in range(4):
            block = repeat * 4 + within
            dilation = 1 + within // 2
            stream_f = stream.astype(jnp.float32)
            hidden = jax.nn.relu(stream_f * gain_outer[block][:, None, None] + bias_outer[block][:, None, None]).astype(jnp.bfloat16)
            hidden = lax.optimization_barrier(hidden).astype(jnp.float32)
            narrow = dilated_conv(hidden, w_narrow[block], dilation)
            inner = jax.nn.relu(narrow * gain_inner[block][:, None, None] + bias_inner[block][:, None, None]).astype(jnp.bfloat16)
            inner = lax.optimization_barrier(inner).astype(jnp.float32)
            widened = dilated_conv(inner, w_widen[block], dilation)
            stream = (stream_f + widened).astype(jnp.bfloat16)
    return stream
```

```python
import functools

import jax
import jax.numpy as jnp
from jax import lax
from jax.experimental import pallas as pl
from jax.experimental.pallas import tpu as pltpu
from jax.sharding import PartitionSpec as P

F32=jnp.float32; BF=jnp.bfloat16
PAD=8

def split(n, umax):
    k = -(-n // umax)
    return k, -(-n // k)

def net_kernel(meta, own_ref, a_ref, b_ref, wn_ref, ww_ref, go_ref, bo_ref, gi_ref, bi_ref, out_ref,
               s_ref, t_ref, h_ref, i_ref, *, R, side, halo, U):
    parity = meta[0]
    g0 = meta[1]
    W = own_ref.shape[-1]
    C = own_ref.shape[1]
    M = wn_ref.shape[2] // 3
    ext = a_ref.shape[0]
    two = own_ref.shape[0]
    base = R * parity
    off_a = jnp.where(parity == 0, 0, ext + two)
    off_b = jnp.where(parity == 0, ext + two, 0)
    lane = lax.broadcasted_iota(jnp.int32, (1, W), 1)

    def valid(y):
        g = g0 + y
        return (g >= 0) & (g < side)

    def right(h, d):
        return jnp.where(lane >= d, pltpu.roll(h, d, 1), 0)

    def left(h, d):
        return jnp.where(lane < W - d, pltpu.roll(h, W - d, 1), 0)

    def sweep(fn, a, n):
        k, u = split(n // 2, U)
        if k == 1:
            for v in range(u):
                fn(a + 2 * v)
            return
        def body(i, _):
            for v in range(u):
                fn(a + 2 * (i * u + v))
            return 0
        lax.fori_loop(0, k, body, 0)

    def hidden(t, y, go, bo):
        h = jnp.maximum(t * go + bo, 0.0)
        return jnp.where(valid(y), h, 0.0).astype(BF)

    def run_pass(ps, tb, lo, n, first):
        for j in range(4):
            d = 1 + j // 2
            gi = gi_ref[ps, j]; bi = bi_ref[ps, j]
            wn = wn_ref[ps, j]; ww = ww_ref[ps, j]
            if j < 3:
                go = go_ref[ps, j + 1]; bo = bo_ref[ps, j + 1]

            def narrow(y):
                rhs = jnp.concatenate(
                    [jnp.concatenate([h_ref[y + r + (k - 1) * d] for k in range(3)], axis=0) for r in range(2)], axis=1)
                p = jnp.dot(wn, rhs, preferred_element_type=F32)
                for r in range(2):
                    q = p[:, r * W:(r + 1) * W]
                    v = right(q[0:M], d) + q[M:2 * M] + left(q[2 * M:3 * M], d)
                    v = jnp.where(valid(y + r), jnp.maximum(v * gi + bi, 0.0), 0.0)
                    i_ref[y + r, 0:M] = right(v, d).astype(BF)
                    i_ref[y + r, M:2 * M] = v.astype(BF)
                    i_ref[y + r, 2 * M:3 * M] = left(v, d).astype(BF)

            def widen(y):
                rhs = jnp.concatenate(
                    [jnp.concatenate([i_ref[y + r + (k - 1) * d] for k in range(3)], axis=0) for r in range(2)], axis=1)
                q = jnp.dot(ww, rhs, preferred_element_type=F32)
                for r in range(2):
                    old = s_ref[y + r] if j == 0 else t_ref[tb, y + r]
                    t = old + q[:, r * W:(r + 1) * W]
                    t_ref[tb, y + r] = t
                    if j < 3:
                        h_ref[y + r] = hidden(t, y + r, go, bo)

            sweep(narrow, lo + d, n - 2 * d)
            sweep(widen, lo + 2 * d, n - 4 * d)
            lo, n = lo + 2 * d, n - 4 * d

    for i in range(ext):
        s_ref[off_a + i] = a_ref[i].astype(F32)
        s_ref[off_b + i] = b_ref[i].astype(F32)
    for i in range(two):
        s_ref[ext + i] = own_ref[i].astype(F32)

    @pl.loop(0, 2)
    def _(ps):
        go = go_ref[0, 0]; bo = bo_ref[0, 0]
        def first(y):
            for r in range(2):
                h_ref[y + r] = hidden(s_ref[y + r], y + r, go, bo)
        sweep(first, base, R + 2 * halo)
        run_pass(ps, ps, base, R + 2 * halo, True)
    h2 = halo // 2
    mid = base + h2
    go = go_ref[2, 0]; bo = bo_ref[2, 0]
    def average(y):
        for r in range(2):
            t = (t_ref[0, y + r] + t_ref[1, y + r]) * 0.5
            s_ref[y + r] = t
            h_ref[y + r] = hidden(t, y + r, go, bo)
    sweep(average, mid, R + halo)
    run_pass(2, 0, mid, R + halo, False)
    for i in range(R):
        out_ref[i] = t_ref[0, base + halo + i].astype(BF)


def net(meta, own, a, b, wn, ww, go, bo, gi, bi, *, R, side, halo, U=3):
    two, C, W = own.shape
    win = two + 2 * a.shape[0] + PAD
    M = wn.shape[2] // 3
    full = lambda: pl.BlockSpec(memory_space=pltpu.VMEM)
    return pl.pallas_call(
        functools.partial(net_kernel, R=R, side=side, halo=halo, U=U),
        out_shape=jax.ShapeDtypeStruct((R, C, W), BF),
        in_specs=[pl.BlockSpec(memory_space=pltpu.SMEM)] + [full() for _ in range(9)],
        out_specs=full(),
        scratch_shapes=[pltpu.VMEM((win, C, W), F32), pltpu.VMEM((2, win, C, W), F32),
                        pltpu.VMEM((win, C, W), BF), pltpu.VMEM((win, 3 * M, W), BF)],
        compiler_params=pltpu.CompilerParams(vmem_limit_bytes=60 * 1024 * 1024),
        name="net",
    )(meta, own, a, b, wn, ww, go, bo, gi, bi)

def prep(go, bo, wn, gi, bi, ww):
    B = wn.shape[0]; M = wn.shape[1]; C = wn.shape[2] // 9
    n = wn.reshape(B, M, 3, 3, C)
    w = ww.reshape(B, C, 3, 3, M)
    n0 = n.transpose(0, 3, 1, 2, 4).reshape(B, 3 * M, 3 * C)
    n1 = n[:4].transpose(0, 2, 1, 3, 4).reshape(4, 3 * M, 3 * C)
    w0 = ww
    w1 = w[:4].transpose(0, 1, 3, 2, 4).reshape(4, C, 9 * M)
    pk = lambda v: jnp.stack([v[:4], v[:4], v[4:]])[..., None]
    return (jnp.stack([n0[:4], n1, n0[4:]]), jnp.stack([w0[:4], w1, w0[4:]]), pk(go), pk(bo), pk(gi), pk(bi))


def send_kernel(x_ref, out_ref):
    C, R, W = x_ref.shape
    pairs = out_ref.shape[0]
    cols = W // pairs
    half = cols // 2
    x = x_ref[...].astype(F32)
    rows = lax.broadcasted_iota(jnp.int32, (W // 2, W), 0)
    lanes = lax.broadcasted_iota(jnp.int32, (W // 2, W), 1)
    for y in range(R):
        plane = x[:, y].astype(BF)
        parts = []
        for lo in range(2):
            pick = (lanes == 2 * rows + lo).astype(F32).astype(BF)
            parts.append(lax.dot_general(pick, plane, (((1,), (1,)), ((), ())), preferred_element_type=F32))
        both = jnp.concatenate(parts, axis=1).astype(BF)
        for q in range(pairs):
            out_ref[q, y * half:(y + 1) * half] = both[q * half:(q + 1) * half]


def join_kernel(meta, recv_ref, x_ref, mate_ref, out_ref):
    n, r, lanes = recv_ref.shape
    C, R, W = x_ref.shape
    half = r // R
    recv = recv_ref[...].reshape(n * r, lanes)
    row = lax.broadcasted_iota(jnp.int32, (n * r, W), 0)
    col = lax.broadcasted_iota(jnp.int32, (n * r, W), 1)
    mine = x_ref[...].astype(F32)
    mate = mate_ref[...].astype(F32)
    first = meta[0] == 0
    for p in range(half):
        pick = (row == col * half + p).astype(F32).astype(BF)
        part = lax.dot_general(recv, pick, (((0,), (0,)), ((), ())), preferred_element_type=F32)
        for lo in range(2):
            y = 2 * p + lo
            own = mine[:, y % R]
            other = mate[:, y % R]
            if y < R:
                straight = jnp.where(first, own, other)
            else:
                straight = jnp.where(first, other, own)
            out_ref[y] = ((straight + part[lo * C:(lo + 1) * C]) * 0.5).astype(BF)


def vmem_call(kernel, out_shape, args, smem=0, name=None):
    return pl.pallas_call(
        kernel,
        out_shape=out_shape,
        in_specs=[pl.BlockSpec(memory_space=pltpu.SMEM)] * smem + [pl.BlockSpec(memory_space=pltpu.VMEM)] * (len(args) - smem),
        out_specs=pl.BlockSpec(memory_space=pltpu.VMEM),
        compiler_params=pltpu.CompilerParams(vmem_limit_bytes=60 * 1024 * 1024),
        name=name,
    )(*args)


def body(features_in, gain_outer, bias_outer, w_narrow, gain_inner, bias_inner, w_widen):
    x = features_in
    C, R, part_cols = x.shape
    n = lax.axis_size("row")
    cols = lax.axis_size("col")
    if cols > 1:
        x = lax.all_gather(x, "col", axis=2, tiled=True)
    W = x.shape[2]
    side = R * n
    pairs = n // 2
    halo = 24
    ops = -(-halo // (2 * R))
    me = lax.axis_index("row")
    parity = me % 2
    meta = jnp.stack([parity, (me - parity) * R - ops * 2 * R]).astype(jnp.int32)
    weights = prep(gain_outer, bias_outer, w_narrow, gain_inner, bias_inner, w_widen)

    swap = [(i, i ^ 1) for i in range(n)]
    mate = lax.ppermute(x, "row", swap)
    sent = vmem_call(send_kernel, jax.ShapeDtypeStruct((pairs, R * R, 2 * C), BF), [x], name="send")
    sent = jnp.broadcast_to(sent[:, None], (pairs, 2) + sent.shape[1:]).reshape((n,) + sent.shape[1:])
    recv = lax.all_to_all(sent, "row", split_axis=0, concat_axis=0, tiled=True)
    own = vmem_call(join_kernel, jax.ShapeDtypeStruct((2 * R, C, W), BF), [meta, recv, x, mate], smem=1, name="join")

    got = []
    for k in range(1, ops + 1):
        hop = [(i, i + 2 * k - 1) for i in range(n) if i % 2 == 1 and i + 2 * k - 1 < n]
        hop += [(i, i - 2 * k + 1) for i in range(n) if i % 2 == 0 and i - 2 * k + 1 >= 0]
        got.append(lax.ppermute(own, "row", hop))
    up = jnp.concatenate(got, axis=0)
    down = jnp.concatenate(got[::-1], axis=0)
    side_rows = jnp.where(parity == 0, down, up)
    other_rows = lax.ppermute(side_rows, "row", swap)
    out = net(meta, own, side_rows, other_rows, *weights, R=R, side=side, halo=halo, U=13)
    out = out.transpose(1, 0, 2)
    if cols > 1:
        out = lax.dynamic_slice_in_dim(out, lax.axis_index("col") * part_cols, part_cols, axis=2)
    return out


def solution(mesh):
    in_specs = (P(None, ("groups", "row"), "col"), P(), P(), P(), P(), P(), P())
    out_specs = P(None, ("groups", "row"), "col")
    return jax.shard_map(body, mesh=mesh, in_specs=in_specs, out_specs=out_specs, check_vma=False)
```

```python
import functools

import jax
import jax.numpy as jnp
from jax import lax
from jax.experimental import pallas as pl
from jax.experimental.pallas import tpu as pltpu
from jax.sharding import PartitionSpec as P

F32=jnp.float32; BF=jnp.bfloat16
LAG=6


def emission(n, lag):
    events = []
    start = 0
    for j in range(4):
        d = 1 + j // 2
        na, nb = n // 2 - d, n // 2 - 2 * d
        for p in range(na):
            events.append((start + p, 1, j, p, "narrow"))
        for q in range(nb):
            events.append((start + q + d + lag, 0, j, q, "widen"))
        nd = 1 + (j + 1) // 2
        start = max(start + na, start + d + lag + nd + 1)
        n -= 4 * d
    return [(j, p, kind) for _, _, j, p, kind in sorted(events, key=lambda e: e[:2])]


def net_kernel(own_ref, a_ref, b_ref, wn_ref, ww_ref, wt_ref, po_ref, pi_ref, out_ref,
               s_ref, t_ref, h_ref, i_ref, *, R, side, halo, lag):
    me = lax.axis_index("row")
    parity = lax.rem(me, 2)
    g0 = (me - parity) * R - a_ref.shape[0]
    W = own_ref.shape[-1]
    C = own_ref.shape[1]
    M = wn_ref.shape[1] // 3
    ext = a_ref.shape[0]
    two = own_ref.shape[0]
    base = R
    shift = R - R * parity
    lane = lax.broadcasted_iota(jnp.int32, (1, W), 1)

    def valid(y):
        g = g0 + y - shift
        return (g >= 0) & (g < side)

    def right(h, d):
        return jnp.where(lane >= d, pltpu.roll(h, d, 1), 0)

    def left(h, d):
        return jnp.where(lane < W - d, pltpu.roll(h, W - d, 1), 0)

    def hidden(t, y, k):
        h = jnp.maximum(t * po_ref[k, 0:C] + po_ref[k, C:2 * C], 0.0)
        return jnp.where(valid(y), h, 0.0).astype(BF)

    def run_pass(tb, lo, n, narrow_row, widen_of, block0):
        los = []
        at = lo
        for j in range(4):
            los.append(at)
            at = at + 2 * (1 + j // 2)

        def narrow(j, y):
            d = 1 + j // 2
            rhs = jnp.concatenate(
                [jnp.concatenate([h_ref[y + r + (k - 1) * d] for k in range(3)], axis=0) for r in range(2)], axis=1)
            p = jnp.dot(wn_ref[narrow_row + j], rhs, preferred_element_type=F32)
            gi = pi_ref[block0 + j, 0:M]
            bi = pi_ref[block0 + j, M:2 * M]
            for r in range(2):
                q = p[:, r * W:(r + 1) * W]
                v = right(q[0:M], d) + q[M:2 * M] + left(q[2 * M:3 * M], d)
                v = jnp.where(valid(y + r), jnp.maximum(v * gi + bi, 0.0), 0.0)
                i_ref[y + r, 0:M] = right(v, d).astype(BF)
                i_ref[y + r, M:2 * M] = v.astype(BF)
                i_ref[y + r, 2 * M:3 * M] = left(v, d).astype(BF)

        def widen(j, y):
            d = 1 + j // 2
            rhs = jnp.concatenate(
                [jnp.concatenate([i_ref[y + r + (k - 1) * d] for k in range(3)], axis=0) for r in range(2)], axis=1)
            q = jnp.dot(widen_of(j), rhs, preferred_element_type=F32)
            for r in range(2):
                old = s_ref[y + r] if j == 0 else t_ref[tb, y + r]
                t = old + q[:, r * W:(r + 1) * W]
                t_ref[tb, y + r] = t
                if j < 3:
                    h_ref[y + r] = hidden(t, y + r, block0 + j + 1)

        for j, p, kind in emission(n, lag):
            d = 1 + j // 2
            if kind == "narrow":
                narrow(j, los[j] + d + 2 * p)
            else:
                widen(j, los[j] + 2 * d + 2 * p)

    pairs = ext // two
    for k in range(pairs):
        at_a = jnp.where(parity == 0, pairs - 1 - k, pairs + 1 + k) * two
        at_b = jnp.where(parity == 0, pairs + 1 + k, pairs - 1 - k) * two
        for i in range(two):
            s_ref[at_a + shift + i] = a_ref[k * two + i].astype(F32)
            s_ref[at_b + shift + i] = b_ref[k * two + i].astype(F32)
    for i in range(two):
        s_ref[ext + shift + i] = own_ref[i].astype(F32)

    @pl.loop(0, 2)
    def _(ps):
        for i in range(R + 2 * halo):
            h_ref[base + i] = hidden(s_ref[base + i], base + i, 0)
        run_pass(ps, base, R + 2 * halo, 4 * ps, lambda j: wt_ref[4 * ps + j], 0)
    mid = base + halo // 2
    for i in range(R + halo):
        t = (t_ref[0, mid + i] + t_ref[1, mid + i]) * 0.5
        s_ref[mid + i] = t
        h_ref[mid + i] = hidden(t, mid + i, 4)
    run_pass(0, mid, R + halo, 8, lambda j: ww_ref[4 + j], 4)
    for i in range(R):
        out_ref[:, i] = t_ref[0, base + halo + i].astype(BF)


def net(own, a, b, wn, ww, wt, po, pi, *, R, side, halo, U=LAG):
    two, C, W = own.shape
    win = two + 2 * a.shape[0] + R
    M = wn.shape[1] // 3
    full = lambda: pl.BlockSpec(memory_space=pltpu.VMEM)
    return pl.pallas_call(
        functools.partial(net_kernel, R=R, side=side, halo=halo, lag=U),
        out_shape=jax.ShapeDtypeStruct((C, R, W), BF),
        in_specs=[full() for _ in range(8)],
        out_specs=full(),
        scratch_shapes=[pltpu.VMEM((win, C, W), F32), pltpu.VMEM((2, win, C, W), F32),
                        pltpu.VMEM((win, C, W), BF), pltpu.VMEM((win, 3 * M, W), BF)],
        compiler_params=pltpu.CompilerParams(vmem_limit_bytes=min(15 * W // 128, 60) * 1024 * 1024),
        name="net",
    )(own, a, b, wn, ww, wt, po, pi)


def prep_kernel(go_ref, bo_ref, wn_ref, gi_ref, bi_ref, ww_ref, n_ref, t_ref, po_ref, pi_ref):
    B, C = go_ref.shape
    M = gi_ref.shape[1]
    W = po_ref.shape[2]
    half = B // 2
    for k in range(B):
        w = wn_ref[k].astype(F32)
        row = k if k < half else k + half
        for kx in range(3):
            n_ref[row, kx * M:(kx + 1) * M] = jnp.concatenate(
                [w[:, (3 * ky + kx) * C:(3 * ky + kx + 1) * C] for ky in range(3)], axis=1).astype(BF)
            if k < half:
                n_ref[k + half, kx * M:(kx + 1) * M] = w[:, 3 * kx * C:3 * (kx + 1) * C].astype(BF)
        if k < half:
            v = ww_ref[k]
            t_ref[k] = v
            v = v.astype(F32)
            t_ref[k + half] = jnp.concatenate(
                [v[:, (3 * kx + ky) * M:(3 * kx + ky + 1) * M] for ky in range(3) for kx in range(3)], axis=1).astype(BF)
    outer = jnp.concatenate([go_ref[...], bo_ref[...]], axis=1).T
    inner = jnp.concatenate([gi_ref[...], bi_ref[...]], axis=1).T
    for k in range(B):
        po_ref[k] = jnp.broadcast_to(outer[:, k:k + 1], (2 * C, W))
        pi_ref[k] = jnp.broadcast_to(inner[:, k:k + 1], (2 * M, W))


def prep(go, bo, wn, gi, bi, ww, W=128):
    B, C = go.shape
    M = gi.shape[1]
    out = (jax.ShapeDtypeStruct((B + B // 2, 3 * M, 3 * C), BF), jax.ShapeDtypeStruct((B, C, 9 * M), BF),
           jax.ShapeDtypeStruct((B, 2 * C, W), F32), jax.ShapeDtypeStruct((B, 2 * M, W), F32))
    n, t, po, pi = pl.pallas_call(
        prep_kernel,
        out_shape=out,
        in_specs=[pl.BlockSpec(memory_space=pltpu.VMEM)] * 6,
        out_specs=[pl.BlockSpec(memory_space=pltpu.VMEM)] * 4,
        compiler_params=pltpu.CompilerParams(vmem_limit_bytes=min(8 * W // 128, 60) * 1024 * 1024),
        name="prep",
    )(go, bo, wn, gi, bi, ww)
    return n, ww, t, po, pi


def send_kernel(x_ref, out_ref):
    C, R, W = x_ref.shape
    pairs = out_ref.shape[0] // 2
    cols = W // pairs
    half = cols // 2
    x = x_ref[...].astype(F32)
    rows = lax.broadcasted_iota(jnp.int32, (W // 2, W), 0)
    lanes = lax.broadcasted_iota(jnp.int32, (W // 2, W), 1)
    for y in range(R):
        plane = x[:, y].astype(BF)
        parts = []
        for lo in range(2):
            pick = (lanes == 2 * rows + lo).astype(F32).astype(BF)
            parts.append(lax.dot_general(pick, plane, (((1,), (1,)), ((), ())), preferred_element_type=F32))
        both = jnp.concatenate(parts, axis=1).astype(BF)
        for q in range(pairs):
            for core in range(2):
                out_ref[2 * q + core, y * half:(y + 1) * half] = both[q * half:(q + 1) * half]


def join_kernel(recv_ref, x_ref, mate_ref, out_ref):
    n, r, lanes = recv_ref.shape
    C, R, W = x_ref.shape
    half = r // R
    recv = recv_ref[...].reshape(n * r, lanes)
    row = lax.broadcasted_iota(jnp.int32, (n * r, W), 0)
    col = lax.broadcasted_iota(jnp.int32, (n * r, W), 1)
    mine = x_ref[...].astype(F32)
    mate = mate_ref[...].astype(F32)
    first = lax.rem(lax.axis_index("row"), 2) == 0
    for p in range(half):
        pick = (row == col * half + p).astype(F32).astype(BF)
        part = lax.dot_general(recv, pick, (((0,), (0,)), ((), ())), preferred_element_type=F32)
        for lo in range(2):
            y = 2 * p + lo
            own = mine[:, y % R]
            other = mate[:, y % R]
            if y < R:
                straight = jnp.where(first, own, other)
            else:
                straight = jnp.where(first, other, own)
            out_ref[y] = ((straight + part[lo * C:(lo + 1) * C]) * 0.5).astype(BF)


def vmem_call(kernel, out_shape, args, name, mib):
    return pl.pallas_call(
        kernel,
        out_shape=out_shape,
        in_specs=[pl.BlockSpec(memory_space=pltpu.VMEM)] * len(args),
        out_specs=pl.BlockSpec(memory_space=pltpu.VMEM),
        compiler_params=pltpu.CompilerParams(vmem_limit_bytes=min(mib, 60) * 1024 * 1024),
        name=name,
    )(*args)


def body(features_in, gain_outer, bias_outer, w_narrow, gain_inner, bias_inner, w_widen):
    x = features_in
    C, R, part_cols = x.shape
    n = lax.axis_size("row")
    cols = lax.axis_size("col")
    if cols > 1:
        x = lax.all_gather(x, "col", axis=2, tiled=True)
    W = x.shape[2]
    side = R * n
    halo = 24
    ops = -(-halo // (2 * R))
    weights = prep(gain_outer, bias_outer, w_narrow, gain_inner, bias_inner, w_widen, W)

    swap = [(i, i ^ 1) for i in range(n)]
    mate = lax.ppermute(x, "row", swap)
    sent = vmem_call(send_kernel, jax.ShapeDtypeStruct((n, R * R, 2 * C), BF), [x], name="send", mib=4 * W // 128)
    recv = lax.all_to_all(sent, "row", split_axis=0, concat_axis=0, tiled=True)
    recv, weights = lax.optimization_barrier((recv, weights))
    own = vmem_call(join_kernel, jax.ShapeDtypeStruct((2 * R, C, W), BF), [recv, x, mate], name="join", mib=4 * W // 128 * W // 128)

    got = []
    for k in range(1, ops + 1):
        hop = [(i, i + 2 * k - 1) for i in range(n) if i % 2 == 1 and i + 2 * k - 1 < n]
        hop += [(i, i - 2 * k + 1) for i in range(n) if i % 2 == 0 and i - 2 * k + 1 >= 0]
        got.append(lax.ppermute(own, "row", hop))
    side_rows = jnp.concatenate(got, axis=0)
    other_rows = lax.ppermute(side_rows, "row", swap)
    out = net(own, side_rows, other_rows, *weights, R=R, side=side, halo=halo)
    if cols > 1:
        out = lax.dynamic_slice_in_dim(out, lax.axis_index("col") * part_cols, part_cols, axis=2)
    return out


def solution(mesh):
    in_specs = (P(None, ("groups", "row"), "col"), P(), P(), P(), P(), P(), P())
    out_specs = P(None, ("groups", "row"), "col")
    return jax.shard_map(body, mesh=mesh, in_specs=in_specs, out_specs=out_specs, check_vma=False)
```

```python
import functools

import jax
import jax.numpy as jnp
from jax import lax
from jax.experimental import pallas as pl
from jax.experimental.pallas import tpu as pltpu
from jax.sharding import PartitionSpec as P

F32 = jnp.float32
BF = jnp.bfloat16
ROWS = 8
LAG = 1
GAP_A = 1
GAP_B = 1


def groups(n):
    return [(at, min(ROWS, n - at)) for at in range(0, n, ROWS)]


def schedule(n, lag):
    parts = []
    done = {}
    lo = 0
    clock = 0
    for j in range(4):
        d = 1 + j // 2
        for name, first, count, gap, late in (
            ("narrow", lo + d, n - 2 * d, GAP_A, 2), ("widen", lo + 2 * d, n - 4 * d, GAP_B, 1)):
            time = clock
            for at, rows in groups(count):
                y = first + at
                reads = range(y - d, y + rows + d)
                source = (j, "narrow") if name == "widen" else (j - 1, "widen")
                ready = max((done.get(source + (r,), -lag) for r in reads), default=0) + lag
                time = max(time + 1, ready)
                for part in range(late + 1):
                    parts.append((time + part * gap, -part, name == "narrow", len(parts), (j, y, rows, name, part)))
                for r in range(y, y + rows):
                    done[(j, name, r)] = time + late * gap
            if name == "narrow":
                clock = time
        lo, n = lo + 2 * d, n - 4 * d
    return [e[-1] for e in sorted(parts)]


def net_kernel(own_ref, far_ref, near_ref, other_ref, wn_ref, ww_ref, wt_ref, po_ref, pi_ref, out_ref,
               s_ref, t_ref, h_ref, i_ref, *, R, side, halo, lag):
    me = lax.axis_index("row")
    parity = lax.rem(me, 2)
    two = near_ref.shape[0]
    pairs = 3
    ext = pairs * two
    g0 = (me - parity) * R - ext
    W = own_ref.shape[-1]
    C = own_ref.shape[1]
    M = wn_ref.shape[1] // 3
    base = R
    shift = R - R * parity
    lane = lax.broadcasted_iota(jnp.int32, (1, W), 1)

    def valid(y):
        g = g0 + y - shift
        return (g >= 0) & (g < side)

    def right(h, d):
        return jnp.where(lane >= d, pltpu.roll(h, d, 1), jnp.zeros_like(h))

    def left(h, d):
        return jnp.where(lane < W - d, pltpu.roll(h, W - d, 1), jnp.zeros_like(h))

    def hidden(t, y, k):
        h = jnp.maximum(t + po_ref[k], 0.0).astype(BF)
        return jnp.where(valid(y), h, jnp.zeros_like(h))

    def run_pass(tb, lo, n, narrow_row, widen_of, block0):
        live = {}

        def narrow(j, y, rows):
            d = 1 + j // 2
            rhs = jnp.concatenate(
                [jnp.concatenate([h_ref[y + r + (k - 1) * d] for k in range(3)], axis=0) for r in range(rows)], axis=1)
            p = jnp.dot(wn_ref[narrow_row + j], rhs, preferred_element_type=F32)
            yield
            vs = []
            for r in range(rows):
                q = p[:, r * W:(r + 1) * W]
                v = right(q[0:M], d) + q[M:2 * M] + left(q[2 * M:3 * M], d)
                v = jnp.maximum(v + pi_ref[block0 + j], 0.0).astype(BF)
                vs.append(jnp.where(valid(y + r), v, jnp.zeros_like(v)))
            yield
            for r in range(rows):
                v = vs[r]
                i_ref[y + r, 0:M] = right(v, d)
                i_ref[y + r, M:2 * M] = v
                i_ref[y + r, 2 * M:3 * M] = left(v, d)

        def widen(j, y, rows):
            d = 1 + j // 2
            rhs = jnp.concatenate(
                [jnp.concatenate([i_ref[y + r + (k - 1) * d] for k in range(3)], axis=0) for r in range(rows)], axis=1)
            q = jnp.dot(widen_of(j), rhs, preferred_element_type=F32)
            yield
            for r in range(rows):
                old = s_ref[y + r] if j == 0 else t_ref[tb, y + r]
                t = old + q[:, r * W:(r + 1) * W]
                t_ref[tb, y + r] = t
                if j < 3:
                    h_ref[y + r] = hidden(t, y + r, block0 + j + 1)

        for j, y, rows, name, part in schedule(n, lag):
            key = (j, y, name)
            if part == 0:
                live[key] = (narrow if name == "narrow" else widen)(j, lo + y, rows)
            next(live[key], None)

    def place(offset, ref, first):
        at = (pairs + offset) * two + shift
        for i in range(two):
            s_ref[at + i] = ref[first + i].astype(F32)

    way = 2 * parity - 1
    place(0, own_ref, 0)
    place(way, own_ref, two)
    place(2 * way, far_ref, 0)
    place(3 * way, far_ref, two)
    place(-way, near_ref, 0)
    place(-2 * way, other_ref, 0)
    place(-3 * way, other_ref, two)

    @pl.loop(0, 2)
    def _(ps):
        for i in range(R + 2 * halo):
            h_ref[base + i] = hidden(s_ref[base + i], base + i, 0)
        run_pass(ps, base, R + 2 * halo, 4 * ps, lambda j: wt_ref[4 * ps + j], 0)
    mid = base + halo // 2
    for i in range(R + halo):
        t = (t_ref[0, mid + i] + t_ref[1, mid + i]) * 0.5
        s_ref[mid + i] = t
        h_ref[mid + i] = hidden(t, mid + i, 4)
    run_pass(0, mid, R + halo, 8, lambda j: ww_ref[4 + j], 4)
    for i in range(R):
        out_ref[:, i] = t_ref[0, base + halo + i].astype(BF)


def net(own, far, near, other, wn, ww, wt, po, pi, *, R, side, halo):
    two, C, W = near.shape
    win = 7 * two + R
    M = wn.shape[1] // 3
    full = lambda: pl.BlockSpec(memory_space=pltpu.VMEM)
    return pl.pallas_call(
        functools.partial(net_kernel, R=R, side=side, halo=halo, lag=LAG),
        out_shape=jax.ShapeDtypeStruct((C, R, W), BF),
        in_specs=[full() for _ in range(9)],
        out_specs=full(),
        scratch_shapes=[pltpu.VMEM((win, C, W), F32), pltpu.VMEM((2, win, C, W), F32),
                        pltpu.VMEM((win, C, W), BF), pltpu.VMEM((win, 3 * M, W), BF)],
        compiler_params=pltpu.CompilerParams(vmem_limit_bytes=min(15 * W // 128, 60) * 1024 * 1024),
        name="net",
    )(own, far, near, other, wn, ww, wt, po, pi)


def prep_kernel(go_ref, bo_ref, wn_ref, gi_ref, bi_ref, ww_ref, n_ref, t_ref, po_ref, pi_ref):
    B, C = go_ref.shape
    M = gi_ref.shape[1]
    W = po_ref.shape[2]
    half = B // 2
    go = go_ref[...]
    outer = (bo_ref[...] / go).T
    inner = bi_ref[...].T
    gain = gi_ref[...].T
    for k in range(B):
        row = k if k < half else k + half
        go3 = jnp.concatenate([go[k:k + 1]] * 9, axis=1)
        w = wn_ref[k].astype(F32) * gain[:, k:k + 1] * go3
        for kx in range(3):
            n_ref[row, kx * M:(kx + 1) * M] = jnp.concatenate(
                [w[:, (3 * ky + kx) * C:(3 * ky + kx + 1) * C] for ky in range(3)], axis=1).astype(BF)
            if k < half:
                n_ref[k + half, kx * M:(kx + 1) * M] = w[:, 3 * kx * C:3 * (kx + 1) * C].astype(BF)
        if k < half:
            v = ww_ref[k]
            t_ref[k] = v
            v = v.astype(F32)
            t_ref[k + half] = jnp.concatenate(
                [v[:, (3 * kx + ky) * M:(3 * kx + ky + 1) * M] for ky in range(3) for kx in range(3)], axis=1).astype(BF)
        po_ref[k] = jnp.broadcast_to(outer[:, k:k + 1], (C, W))
        pi_ref[k] = jnp.broadcast_to(inner[:, k:k + 1], (M, W))


def prep(go, bo, wn, gi, bi, ww, W=128):
    B, C = go.shape
    M = gi.shape[1]
    out = (jax.ShapeDtypeStruct((B + B // 2, 3 * M, 3 * C), BF), jax.ShapeDtypeStruct((B, C, 9 * M), BF),
           jax.ShapeDtypeStruct((B, C, W), F32), jax.ShapeDtypeStruct((B, M, W), F32))
    n, t, po, pi = pl.pallas_call(
        prep_kernel,
        out_shape=out,
        in_specs=[pl.BlockSpec(memory_space=pltpu.VMEM)] * 6,
        out_specs=[pl.BlockSpec(memory_space=pltpu.VMEM)] * 4,
        compiler_params=pltpu.CompilerParams(vmem_limit_bytes=min(8 * W // 128, 60) * 1024 * 1024),
        name="prep",
    )(go, bo, wn, gi, bi, ww)
    return n, ww, t, po, pi


def send_kernel(x_ref, out_ref):
    C, R, W = x_ref.shape
    pairs = out_ref.shape[0] // 2
    cols = W // pairs
    half = cols // 2
    block = R * half
    x = x_ref[...].astype(F32)
    rows = lax.broadcasted_iota(jnp.int32, (W // 2, W), 0)
    lanes = lax.broadcasted_iota(jnp.int32, (W // 2, W), 1)
    picks = [(lanes == 2 * rows + lo).astype(F32).astype(BF) for lo in range(2)]
    nothing = jnp.zeros((block, 2 * C), BF)
    out_ref[0, block:2 * block] = nothing
    out_ref[2 * pairs - 1, block:2 * block] = nothing
    for y in range(R):
        plane = x[:, y].astype(BF)
        parts = [lax.dot_general(pick, plane, (((1,), (1,)), ((), ())), preferred_element_type=F32) for pick in picks]
        both = jnp.concatenate(parts, axis=1).astype(BF)
        for q in range(pairs):
            piece = both[q * half:(q + 1) * half]
            at = y * half
            out_ref[2 * q, at:at + half] = piece
            out_ref[2 * q + 1, at:at + half] = piece
            if q + 1 < pairs:
                out_ref[2 * q + 2, block + at:block + at + half] = piece
            if q > 0:
                out_ref[2 * q - 1, block + at:block + at + half] = piece


def join_kernel(recv_ref, mine_ref, next_ref, out_ref, near_ref):
    n, r, lanes = recv_ref.shape
    _, C, R, W = mine_ref.shape
    block = r // 2
    half = block // R
    row = lax.broadcasted_iota(jnp.int32, (n * block, W), 0)
    col = lax.broadcasted_iota(jnp.int32, (n * block, W), 1)
    even = lax.rem(lax.axis_index("row"), 2) == 0
    picks = [(row == col * half + p).astype(F32).astype(BF) for p in range(half)]
    for which, rows_ref in enumerate((mine_ref, next_ref)):
        recv = recv_ref[:, which * block:(which + 1) * block].reshape(n * block, lanes)
        first = rows_ref[0].astype(F32)
        second = rows_ref[1].astype(F32)
        ahead = even if which == 0 else jnp.logical_not(even)
        for p in range(half):
            part = lax.dot_general(recv, picks[p], (((0,), (0,)), ((), ())), preferred_element_type=F32)
            for lo in range(2):
                y = 2 * p + lo
                a, b = first[:, y % R], second[:, y % R]
                straight = jnp.where(ahead, a, b) if y < R else jnp.where(ahead, b, a)
                out = ((straight + part[lo * C:(lo + 1) * C]) * 0.5).astype(BF)
                out_ref[which * 2 * R + y] = out
                if which == 1:
                    near_ref[y] = out


def vmem_call(kernel, out_shape, args, name, mib):
    return pl.pallas_call(
        kernel,
        out_shape=out_shape,
        in_specs=[pl.BlockSpec(memory_space=pltpu.VMEM)] * len(args),
        out_specs=jax.tree.map(lambda _: pl.BlockSpec(memory_space=pltpu.VMEM), out_shape),
        compiler_params=pltpu.CompilerParams(vmem_limit_bytes=min(mib, 60) * 1024 * 1024),
        name=name,
    )(*args)


def body(features_in, gain_outer, bias_outer, w_narrow, gain_inner, bias_inner, w_widen):
    x = features_in
    C, R, part_cols = x.shape
    n = lax.axis_size("row")
    cols = lax.axis_size("col")
    if cols > 1:
        x = lax.all_gather(x, "col", axis=2, tiled=True)
    W = x.shape[2]
    side = R * n
    halo = 24
    assert halo <= 6 * R and n % 2 == 0
    weights = prep(gain_outer, bias_outer, w_narrow, gain_inner, bias_inner, w_widen, W)

    swap = [(i, i ^ 1) for i in range(n)]
    beside = [(i, i + 1) for i in range(1, n - 1, 2)] + [(i, i - 1) for i in range(2, n, 2)]
    beyond = [(i, i + 4) for i in range(0, n - 4, 2)] + [(i, i - 4) for i in range(5, n, 2)]
    mate = lax.ppermute(x, "row", swap)
    mine = jnp.stack([x, mate])
    following = lax.ppermute(mine, "row", beside)
    sent = vmem_call(send_kernel, jax.ShapeDtypeStruct((n, 2 * R * R, 2 * C), BF), [x], name="send", mib=4 * W // 128)
    recv = lax.all_to_all(sent, "row", split_axis=0, concat_axis=0, tiled=True)
    recv, weights = lax.optimization_barrier((recv, weights))
    rows = lambda k: jax.ShapeDtypeStruct((k * R, C, W), BF)
    own, near = vmem_call(join_kernel, (rows(4), rows(2)), [recv, mine, following], name="join", mib=6 * W // 128 * W // 128)
    far = lax.ppermute(own, "row", beyond)
    near = lax.ppermute(near, "row", swap)
    other = lax.ppermute(far, "row", swap)
    out = net(own, far, near, other, *weights, R=R, side=side, halo=halo)
    if cols > 1:
        out = lax.dynamic_slice_in_dim(out, lax.axis_index("col") * part_cols, part_cols, axis=2)
    return out


def solution(mesh):
    in_specs = (P(None, ("groups", "row"), "col"), P(), P(), P(), P(), P(), P())
    out_specs = P(None, ("groups", "row"), "col")
    return jax.shard_map(body, mesh=mesh, in_specs=in_specs, out_specs=out_specs, check_vma=False)
```

```python
import functools

import jax
import jax.numpy as jnp
from jax import lax
from jax.experimental import pallas as pl
from jax.experimental.pallas import tpu as pltpu
from jax.sharding import PartitionSpec as P

F32 = jnp.float32
BF = jnp.bfloat16
ROWS, ROWS2 = 8, 4
LAG = LAG2 = 1
GAP_A = GAP_B = 1
SKEW = 0


def groups(n, rows):
    return [(at, min(rows, n - at)) for at in range(0, n, rows)]


def schedule(total, halo):
    parts = []
    done = {}
    emitted = [0]

    def put(time, which, j, name, y, rows, late, gap):
        for part in range(late + 1):
            parts.append((time + part * gap, -part, name == "narrow", emitted[0], (which, j, y, rows, name, part)))
            emitted[0] += 1
        for r in range(y, y + rows):
            done[(which, j, name, r)] = time + late * gap

    def run(which, lo, n, clock, size, lag):
        for j in range(4):
            d = 1 + j // 2
            for name, first, count in (("narrow", lo + d, n - 2 * d), ("widen", lo + 2 * d, n - 4 * d)):
                time = clock
                for at, rows in groups(count, size):
                    y = first + at
                    source = (which, j, "narrow") if name == "widen" else (which, j - 1, "widen")
                    ready = [done[source + (r,)] + lag for r in range(y - d, y + rows + d) if source + (r,) in done]
                    time = max([time + 1] + ready)
                    if name == "narrow":
                        put(time, which, j, name, y, rows, 2, GAP_A)
                    else:
                        put(time, which, j, name, y, rows, 1, GAP_B)
                if name == "narrow":
                    clock = time
            lo, n = lo + 2 * d, n - 4 * d

    for which in range(2):
        run(which, 0, total, which * SKEW, ROWS, LAG)
    mid, n = halo // 2, total - halo
    time = 0
    for at, rows in groups(n, ROWS2):
        y = mid + at
        time = max([time + 1] + [done[(v, 3, "widen", r)] + 1 for v in range(2) for r in range(y, y + rows)])
        put(time, 2, -1, "widen", y, rows, 0, 0)
    run(2, mid, n, done[(2, -1, "widen", mid)], ROWS2, LAG2)
    return [e[-1] for e in sorted(parts)]


def net_kernel(own_ref, far_ref, near_ref, other_ref, wn_ref, ww_ref, wt_ref, po_ref, pi_ref, out_ref,
               s_ref, t_ref, first_ref, h_ref, i_ref, *, R, side, halo):
    me = lax.axis_index("row")
    parity = lax.rem(me, 2)
    two = near_ref.shape[0]
    pairs = 3
    ext = pairs * two
    g0 = (me - parity) * R - ext
    W = own_ref.shape[-1]
    C = own_ref.shape[1]
    M = wn_ref.shape[1] // 3
    base = R
    shift = R - R * parity
    lane = lax.broadcasted_iota(jnp.int32, (1, W), 1)

    def valid(y):
        g = g0 + y - shift
        return (g >= 0) & (g < side)

    def right(h, d):
        return jnp.where(lane >= d, pltpu.roll(h, d, 1), jnp.zeros_like(h))

    def left(h, d):
        return jnp.where(lane < W - d, pltpu.roll(h, W - d, 1), jnp.zeros_like(h))

    def hidden(t, y, k):
        h = jnp.maximum(t + po_ref[k], 0.0).astype(BF)
        return jnp.where(valid(y), h, jnp.zeros_like(h))

    def narrow(which, j, y, rows):
        d = 1 + j // 2
        hid = first_ref if j == 0 and which < 2 else h_ref.at[which]
        rhs = jnp.concatenate(
            [jnp.concatenate([hid[y + r + (k - 1) * d] for k in range(3)], axis=0) for r in range(rows)], axis=1)
        p = jnp.dot(wn_ref[4 * which + j], rhs, preferred_element_type=F32)
        yield
        vs = []
        block = 4 * (which // 2) + j
        for r in range(rows):
            q = p[:, r * W:(r + 1) * W]
            v = right(q[0:M], d) + q[M:2 * M] + left(q[2 * M:3 * M], d)
            v = jnp.maximum(v + pi_ref[block], 0.0).astype(BF)
            vs.append(jnp.where(valid(y + r), v, jnp.zeros_like(v)))
        yield
        for r in range(rows):
            v = vs[r]
            i_ref[which, y + r, 0:M] = right(v, d)
            i_ref[which, y + r, M:2 * M] = v
            i_ref[which, y + r, 2 * M:3 * M] = left(v, d)

    def widen(which, j, y, rows):
        d = 1 + j // 2
        block = 4 * (which // 2) + j
        rhs = jnp.concatenate(
            [jnp.concatenate([i_ref[which, y + r + (k - 1) * d] for k in range(3)], axis=0) for r in range(rows)], axis=1)
        taps = ww_ref[block] if which == 2 else wt_ref[4 * which + j]
        q = jnp.dot(taps, rhs, preferred_element_type=F32)
        yield
        for r in range(rows):
            old = s_ref[y + r] if j == 0 and which < 2 else t_ref[which, y + r]
            t = old + q[:, r * W:(r + 1) * W]
            t_ref[which, y + r] = t
            if j < 3:
                h_ref[which, y + r] = hidden(t, y + r, block + 1)

    def average(which, j, y, rows):
        for r in range(rows):
            t = (t_ref[0, y + r] + t_ref[1, y + r]) * 0.5
            t_ref[2, y + r] = t
            h_ref[2, y + r] = hidden(t, y + r, 4)
        yield

    def place(offset, ref, first):
        at = (pairs + offset) * two + shift
        for i in range(two):
            s_ref[at + i] = ref[first + i].astype(F32)

    way = 2 * parity - 1
    place(0, own_ref, 0)
    place(way, own_ref, two)
    place(2 * way, far_ref, 0)
    place(3 * way, far_ref, two)
    place(-way, near_ref, 0)
    place(-2 * way, other_ref, 0)
    place(-3 * way, other_ref, two)

    for i in range(R + 2 * halo):
        first_ref[base + i] = hidden(s_ref[base + i], base + i, 0)
    live = {}
    for which, j, y, rows, name, part in schedule(R + 2 * halo, halo):
        key = (which, j, y, name)
        if part == 0:
            step = average if j < 0 else narrow if name == "narrow" else widen
            live[key] = step(which, j, base + y, rows)
        next(live[key], None)
    for i in range(R):
        out_ref[:, i] = t_ref[2, base + halo + i].astype(BF)


def net(own, far, near, other, wn, ww, wt, po, pi, *, R, side, halo):
    two, C, W = near.shape
    win = 7 * two + R
    M = wn.shape[1] // 3
    full = lambda: pl.BlockSpec(memory_space=pltpu.VMEM)
    return pl.pallas_call(
        functools.partial(net_kernel, R=R, side=side, halo=halo),
        out_shape=jax.ShapeDtypeStruct((C, R, W), BF),
        in_specs=[full() for _ in range(9)],
        out_specs=full(),
        scratch_shapes=[pltpu.VMEM((win, C, W), F32), pltpu.VMEM((3, win, C, W), F32), pltpu.VMEM((win, C, W), BF),
                        pltpu.VMEM((3, win, C, W), BF), pltpu.VMEM((3, win, 3 * M, W), BF)],
        compiler_params=pltpu.CompilerParams(vmem_limit_bytes=min(20 * W // 128, 60) * 1024 * 1024),
        name="net",
    )(own, far, near, other, wn, ww, wt, po, pi)


def prep_kernel(go_ref, bo_ref, wn_ref, gi_ref, bi_ref, ww_ref, n_ref, t_ref, po_ref, pi_ref):
    B, C = go_ref.shape
    M = gi_ref.shape[1]
    W = po_ref.shape[2]
    half = B // 2
    go = go_ref[...]
    outer = (bo_ref[...] / go).T
    inner = bi_ref[...].T
    gain = gi_ref[...].T
    for k in range(B):
        row = k if k < half else k + half
        go3 = jnp.concatenate([go[k:k + 1]] * 9, axis=1)
        w = wn_ref[k].astype(F32) * gain[:, k:k + 1] * go3
        for kx in range(3):
            n_ref[row, kx * M:(kx + 1) * M] = jnp.concatenate(
                [w[:, (3 * ky + kx) * C:(3 * ky + kx + 1) * C] for ky in range(3)], axis=1).astype(BF)
            if k < half:
                n_ref[k + half, kx * M:(kx + 1) * M] = w[:, 3 * kx * C:3 * (kx + 1) * C].astype(BF)
        if k < half:
            v = ww_ref[k]
            t_ref[k] = v
            v = v.astype(F32)
            t_ref[k + half] = jnp.concatenate(
                [v[:, (3 * kx + ky) * M:(3 * kx + ky + 1) * M] for ky in range(3) for kx in range(3)], axis=1).astype(BF)
        po_ref[k] = jnp.broadcast_to(outer[:, k:k + 1], (C, W))
        pi_ref[k] = jnp.broadcast_to(inner[:, k:k + 1], (M, W))


def prep(go, bo, wn, gi, bi, ww, W=128):
    B, C = go.shape
    M = gi.shape[1]
    out = (jax.ShapeDtypeStruct((B + B // 2, 3 * M, 3 * C), BF), jax.ShapeDtypeStruct((B, C, 9 * M), BF),
           jax.ShapeDtypeStruct((B, C, W), F32), jax.ShapeDtypeStruct((B, M, W), F32))
    n, t, po, pi = pl.pallas_call(
        prep_kernel,
        out_shape=out,
        in_specs=[pl.BlockSpec(memory_space=pltpu.VMEM)] * 6,
        out_specs=[pl.BlockSpec(memory_space=pltpu.VMEM)] * 4,
        compiler_params=pltpu.CompilerParams(vmem_limit_bytes=min(8 * W // 128, 60) * 1024 * 1024),
        name="prep",
    )(go, bo, wn, gi, bi, ww)
    return n, ww, t, po, pi


def send_kernel(x_ref, out_ref):
    C, R, W = x_ref.shape
    pairs = out_ref.shape[0] // 2
    cols = W // pairs
    half = cols // 2
    block = R * half
    x = x_ref[...].astype(F32)
    rows = lax.broadcasted_iota(jnp.int32, (W // 2, W), 0)
    lanes = lax.broadcasted_iota(jnp.int32, (W // 2, W), 1)
    picks = [(lanes == 2 * rows + lo).astype(F32).astype(BF) for lo in range(2)]
    nothing = jnp.zeros((block, 2 * C), BF)
    out_ref[0, block:2 * block] = nothing
    out_ref[2 * pairs - 1, block:2 * block] = nothing
    for y in range(R):
        plane = x[:, y].astype(BF)
        parts = [lax.dot_general(pick, plane, (((1,), (1,)), ((), ())), preferred_element_type=F32) for pick in picks]
        both = jnp.concatenate(parts, axis=1).astype(BF)
        for q in range(pairs):
            piece = both[q * half:(q + 1) * half]
            at = y * half
            out_ref[2 * q, at:at + half] = piece
            out_ref[2 * q + 1, at:at + half] = piece
            if q + 1 < pairs:
                out_ref[2 * q + 2, block + at:block + at + half] = piece
            if q > 0:
                out_ref[2 * q - 1, block + at:block + at + half] = piece


def join_kernel(recv_ref, mine_ref, next_ref, out_ref, near_ref):
    n, r, lanes = recv_ref.shape
    _, C, R, W = mine_ref.shape
    block = r // 2
    half = block // R
    row = lax.broadcasted_iota(jnp.int32, (n * block, W), 0)
    col = lax.broadcasted_iota(jnp.int32, (n * block, W), 1)
    even = lax.rem(lax.axis_index("row"), 2) == 0
    picks = [(row == col * half + p).astype(F32).astype(BF) for p in range(half)]
    for which, rows_ref in enumerate((mine_ref, next_ref)):
        recv = recv_ref[:, which * block:(which + 1) * block].reshape(n * block, lanes)
        first = rows_ref[0].astype(F32)
        second = rows_ref[1].astype(F32)
        ahead = even if which == 0 else jnp.logical_not(even)
        for p in range(half):
            part = lax.dot_general(recv, picks[p], (((0,), (0,)), ((), ())), preferred_element_type=F32)
            for lo in range(2):
                y = 2 * p + lo
                a, b = first[:, y % R], second[:, y % R]
                straight = jnp.where(ahead, a, b) if y < R else jnp.where(ahead, b, a)
                out = ((straight + part[lo * C:(lo + 1) * C]) * 0.5).astype(BF)
                out_ref[which * 2 * R + y] = out
                if which == 1:
                    near_ref[y] = out


def vmem_call(kernel, out_shape, args, name, mib):
    return pl.pallas_call(
        kernel,
        out_shape=out_shape,
        in_specs=[pl.BlockSpec(memory_space=pltpu.VMEM)] * len(args),
        out_specs=jax.tree.map(lambda _: pl.BlockSpec(memory_space=pltpu.VMEM), out_shape),
        compiler_params=pltpu.CompilerParams(vmem_limit_bytes=min(mib, 60) * 1024 * 1024),
        name=name,
    )(*args)


def body(features_in, gain_outer, bias_outer, w_narrow, gain_inner, bias_inner, w_widen):
    x = features_in
    C, R, part_cols = x.shape
    n = lax.axis_size("row")
    cols = lax.axis_size("col")
    if cols > 1:
        x = lax.all_gather(x, "col", axis=2, tiled=True)
    W = x.shape[2]
    side = R * n
    halo = 24
    assert halo <= 6 * R and n % 2 == 0
    weights = prep(gain_outer, bias_outer, w_narrow, gain_inner, bias_inner, w_widen, W)

    swap = [(i, i ^ 1) for i in range(n)]
    beside = [(i, i + 1) for i in range(1, n - 1, 2)] + [(i, i - 1) for i in range(2, n, 2)]
    beyond = [(i, i + 4) for i in range(0, n - 4, 2)] + [(i, i - 4) for i in range(5, n, 2)]
    mate = lax.ppermute(x, "row", swap)
    mine = jnp.stack([x, mate])
    following = lax.ppermute(mine, "row", beside)
    sent = vmem_call(send_kernel, jax.ShapeDtypeStruct((n, 2 * R * R, 2 * C), BF), [x], name="send", mib=4 * W // 128)
    recv = lax.all_to_all(sent, "row", split_axis=0, concat_axis=0, tiled=True)
    recv, weights = lax.optimization_barrier((recv, weights))
    rows = lambda k: jax.ShapeDtypeStruct((k * R, C, W), BF)
    own, near = vmem_call(join_kernel, (rows(4), rows(2)), [recv, mine, following], name="join", mib=6 * W // 128 * W // 128)
    far = lax.ppermute(own, "row", beyond)
    near = lax.ppermute(near, "row", swap)
    other = lax.ppermute(far, "row", swap)
    out = net(own, far, near, other, *weights, R=R, side=side, halo=halo)
    if cols > 1:
        out = lax.dynamic_slice_in_dim(out, lax.axis_index("col") * part_cols, part_cols, axis=2)
    return out


def solution(mesh):
    in_specs = (P(None, ("groups", "row"), "col"), P(), P(), P(), P(), P(), P())
    out_specs = P(None, ("groups", "row"), "col")
    return jax.shard_map(body, mesh=mesh, in_specs=in_specs, out_specs=out_specs, check_vma=False)
```

```python
import functools

import jax
import jax.numpy as jnp
from jax import lax
from jax.experimental import pallas as pl
from jax.experimental.pallas import tpu as pltpu
from jax.sharding import PartitionSpec as P


F32 = jnp.float32
BF = jnp.bfloat16
ROWS, ROWS2 = 8, 4
LAG = LAG2 = 1
GAP_A = GAP_B = 1
SKEW = 0


def groups(n, rows):
    return [(at, min(rows, n - at)) for at in range(0, n, rows)]


def schedule(total, halo):
    parts = []
    done = {}
    emitted = [0]

    def put(time, which, j, name, y, rows, late, gap):
        for part in range(late + 1):
            parts.append((time + part * gap, -part, name == "narrow", emitted[0], (which, j, y, rows, name, part)))
            emitted[0] += 1
        for r in range(y, y + rows):
            done[(which, j, name, r)] = time + late * gap

    def run(which, lo, n, clock, size, lag):
        for j in range(4):
            d = 1 + j // 2
            for name, first, count in (("narrow", lo + d, n - 2 * d), ("widen", lo + 2 * d, n - 4 * d)):
                time = clock
                for at, rows in groups(count, size):
                    y = first + at
                    source = (which, j, "narrow") if name == "widen" else (which, j - 1, "widen")
                    ready = [done[source + (r,)] + lag for r in range(y - d, y + rows + d) if source + (r,) in done]
                    time = max([time + 1] + ready)
                    if name == "narrow":
                        put(time, which, j, name, y, rows, 2, GAP_A)
                    else:
                        put(time, which, j, name, y, rows, 1, GAP_B)
                if name == "narrow":
                    clock = time
            lo, n = lo + 2 * d, n - 4 * d

    for which in range(2):
        run(which, 0, total, which * SKEW, ROWS, LAG)
    mid, n = halo // 2, total - halo
    time = 0
    for at, rows in groups(n, ROWS2):
        y = mid + at
        time = max([time + 1] + [done[(v, 3, "widen", r)] + 1 for v in range(2) for r in range(y, y + rows)])
        put(time, 2, -1, "widen", y, rows, 0, 0)
    run(2, mid, n, done[(2, -1, "widen", mid)], ROWS2, LAG2)
    return [e[-1] for e in sorted(parts)]


def net_kernel(own_ref, far_ref, near_ref, other_ref, wn_ref, ww_ref, wt_ref, po_ref, pi_ref, out_ref,
               s_ref, t_ref, first_ref, h_ref, i_ref, *, R, side, halo):
    me = lax.axis_index("row")
    parity = lax.rem(me, 2)
    two = near_ref.shape[0]
    pairs = 3
    ext = pairs * two
    g0 = (me - parity) * R - ext
    W = own_ref.shape[-1]
    M = wn_ref.shape[1] // 3
    base = R
    shift = R - R * parity
    lane = lax.broadcasted_iota(jnp.int32, (1, W), 1)

    def valid(y):
        g = g0 + y - shift
        return (g >= 0) & (g < side)

    def right(h, d):
        return jnp.where(lane >= d, pltpu.roll(h, d, 1), jnp.zeros_like(h))

    def left(h, d):
        return jnp.where(lane < W - d, pltpu.roll(h, W - d, 1), jnp.zeros_like(h))

    def hidden(t, y, k):
        h = jnp.maximum(t + po_ref[k], 0.0).astype(BF)
        return jnp.where(valid(y), h, jnp.zeros_like(h))

    def narrow(which, j, y, rows):
        d = 1 + j // 2
        hid = first_ref if j == 0 and which < 2 else h_ref.at[which]
        rhs = jnp.concatenate(
            [jnp.concatenate([hid[y + r + (k - 1) * d] for k in range(3)], axis=0) for r in range(rows)], axis=1)
        p = jnp.dot(wn_ref[4 * which + j], rhs, preferred_element_type=F32)
        yield
        vs = []
        block = 4 * (which // 2) + j
        for r in range(rows):
            q = p[:, r * W:(r + 1) * W]
            v = right(q[0:M], d) + q[M:2 * M] + left(q[2 * M:3 * M], d)
            v = jnp.maximum(v + pi_ref[block], 0.0).astype(BF)
            vs.append(jnp.where(valid(y + r), v, jnp.zeros_like(v)))
        yield
        for r in range(rows):
            v = vs[r]
            i_ref[which, y + r, 0:M] = right(v, d)
            i_ref[which, y + r, M:2 * M] = v
            i_ref[which, y + r, 2 * M:3 * M] = left(v, d)

    def widen(which, j, y, rows):
        d = 1 + j // 2
        block = 4 * (which // 2) + j
        rhs = jnp.concatenate(
            [jnp.concatenate([i_ref[which, y + r + (k - 1) * d] for k in range(3)], axis=0) for r in range(rows)], axis=1)
        taps = ww_ref[block] if which == 2 else wt_ref[4 * which + j]
        q = jnp.dot(taps, rhs, preferred_element_type=F32)
        yield
        for r in range(rows):
            old = s_ref[y + r] if j == 0 and which < 2 else t_ref[which, y + r]
            t = old + q[:, r * W:(r + 1) * W]
            t_ref[which, y + r] = t
            if j < 3:
                h_ref[which, y + r] = hidden(t, y + r, block + 1)

    def average(which, j, y, rows):
        for r in range(rows):
            t = (t_ref[0, y + r] + t_ref[1, y + r]) * 0.5
            t_ref[2, y + r] = t
            h_ref[2, y + r] = hidden(t, y + r, 4)
        yield

    def place(offset, ref, first):
        at = (pairs + offset) * two + shift
        for i in range(two):
            s_ref[at + i] = ref[first + i].astype(F32)

    way = 2 * parity - 1
    place(0, own_ref, 0)
    place(way, own_ref, two)
    place(2 * way, far_ref, 0)
    place(3 * way, far_ref, two)
    place(-way, near_ref, 0)
    place(-2 * way, other_ref, 0)
    place(-3 * way, other_ref, two)

    for i in range(R + 2 * halo):
        first_ref[base + i] = hidden(s_ref[base + i], base + i, 0)
    live = {}
    for which, j, y, rows, name, part in schedule(R + 2 * halo, halo):
        key = (which, j, y, name)
        if part == 0:
            step = average if j < 0 else narrow if name == "narrow" else widen
            live[key] = step(which, j, base + y, rows)
        next(live[key], None)
    for i in range(R):
        out_ref[:, i] = t_ref[2, base + halo + i].astype(BF)


def net(own, far, near, other, wn, ww, wt, po, pi, *, R, side, halo):
    two, C, W = near.shape
    win = 7 * two + R
    M = wn.shape[1] // 3
    full = lambda: pl.BlockSpec(memory_space=pltpu.VMEM)
    return pl.pallas_call(
        functools.partial(net_kernel, R=R, side=side, halo=halo),
        out_shape=jax.ShapeDtypeStruct((C, R, W), BF),
        in_specs=[full() for _ in range(9)],
        out_specs=full(),
        scratch_shapes=[pltpu.VMEM((win, C, W), F32), pltpu.VMEM((3, win, C, W), F32), pltpu.VMEM((win, C, W), BF),
                        pltpu.VMEM((3, win, C, W), BF), pltpu.VMEM((3, win, 3 * M, W), BF)],
        compiler_params=pltpu.CompilerParams(vmem_limit_bytes=min(20 * W // 128, 60) * 1024 * 1024),
        name="net",
    )(own, far, near, other, wn, ww, wt, po, pi)


def prep_kernel(go_ref, bo_ref, wn_ref, gi_ref, bi_ref, ww_ref, n_ref, t_ref, po_ref, pi_ref):
    B, C = go_ref.shape
    M = gi_ref.shape[1]
    W = po_ref.shape[2]
    half = B // 2
    go = go_ref[...]
    outer = (bo_ref[...] / go).T
    inner = bi_ref[...].T
    gain = gi_ref[...].T
    for k in range(B):
        row = k if k < half else k + half
        go3 = jnp.concatenate([go[k:k + 1]] * 9, axis=1)
        w = wn_ref[k].astype(F32) * gain[:, k:k + 1] * go3
        for kx in range(3):
            n_ref[row, kx * M:(kx + 1) * M] = jnp.concatenate(
                [w[:, (3 * ky + kx) * C:(3 * ky + kx + 1) * C] for ky in range(3)], axis=1).astype(BF)
            if k < half:
                n_ref[k + half, kx * M:(kx + 1) * M] = w[:, 3 * kx * C:3 * (kx + 1) * C].astype(BF)
        if k < half:
            v = ww_ref[k]
            t_ref[k] = v
            v = v.astype(F32)
            t_ref[k + half] = jnp.concatenate(
                [v[:, (3 * kx + ky) * M:(3 * kx + ky + 1) * M] for ky in range(3) for kx in range(3)], axis=1).astype(BF)
        po_ref[k] = jnp.broadcast_to(outer[:, k:k + 1], (C, W))
        pi_ref[k] = jnp.broadcast_to(inner[:, k:k + 1], (M, W))


def prep(go, bo, wn, gi, bi, ww, W=128):
    B, C = go.shape
    M = gi.shape[1]
    out = (jax.ShapeDtypeStruct((B + B // 2, 3 * M, 3 * C), BF), jax.ShapeDtypeStruct((B, C, 9 * M), BF),
           jax.ShapeDtypeStruct((B, C, W), F32), jax.ShapeDtypeStruct((B, M, W), F32))
    n, t, po, pi = pl.pallas_call(
        prep_kernel,
        out_shape=out,
        in_specs=[pl.BlockSpec(memory_space=pltpu.VMEM)] * 6,
        out_specs=[pl.BlockSpec(memory_space=pltpu.VMEM)] * 4,
        compiler_params=pltpu.CompilerParams(vmem_limit_bytes=min(8 * W // 128, 60) * 1024 * 1024),
        name="prep",
    )(go, bo, wn, gi, bi, ww)
    return n, ww, t, po, pi


def send_kernel(x_ref, out_ref):
    C, R, W = x_ref.shape
    pairs = out_ref.shape[0] // 2
    cols = W // pairs
    half = cols // 2
    block = R * half
    x = x_ref[...].astype(F32)
    rows = lax.broadcasted_iota(jnp.int32, (W // 2, W), 0)
    lanes = lax.broadcasted_iota(jnp.int32, (W // 2, W), 1)
    picks = [(lanes == 2 * rows + lo).astype(F32).astype(BF) for lo in range(2)]
    nothing = jnp.zeros((block, 2 * C), BF)
    out_ref[0, block:2 * block] = nothing
    out_ref[2 * pairs - 1, block:2 * block] = nothing
    for y in range(R):
        plane = x[:, y].astype(BF)
        parts = [lax.dot_general(pick, plane, (((1,), (1,)), ((), ())), preferred_element_type=F32) for pick in picks]
        both = jnp.concatenate(parts, axis=1).astype(BF)
        for q in range(pairs):
            piece = both[q * half:(q + 1) * half]
            at = y * half
            out_ref[2 * q, at:at + half] = piece
            out_ref[2 * q + 1, at:at + half] = piece
            if q + 1 < pairs:
                out_ref[2 * q + 2, block + at:block + at + half] = piece
            if q > 0:
                out_ref[2 * q - 1, block + at:block + at + half] = piece


def join_kernel(recv_ref, mine_ref, next_ref, out_ref, near_ref):
    n, r, lanes = recv_ref.shape
    _, C, R, W = mine_ref.shape
    block = r // 2
    half = block // R
    row = lax.broadcasted_iota(jnp.int32, (n * block, W), 0)
    col = lax.broadcasted_iota(jnp.int32, (n * block, W), 1)
    even = lax.rem(lax.axis_index("row"), 2) == 0
    picks = [(row == col * half + p).astype(F32).astype(BF) for p in range(half)]
    for which, rows_ref in enumerate((mine_ref, next_ref)):
        recv = recv_ref[:, which * block:(which + 1) * block].reshape(n * block, lanes)
        first = rows_ref[0].astype(F32)
        second = rows_ref[1].astype(F32)
        ahead = even if which == 0 else jnp.logical_not(even)
        for p in range(half):
            part = lax.dot_general(recv, picks[p], (((0,), (0,)), ((), ())), preferred_element_type=F32)
            for lo in range(2):
                y = 2 * p + lo
                a, b = first[:, y % R], second[:, y % R]
                straight = jnp.where(ahead, a, b) if y < R else jnp.where(ahead, b, a)
                out = ((straight + part[lo * C:(lo + 1) * C]) * 0.5).astype(BF)
                out_ref[which * 2 * R + y] = out
                if which == 1:
                    near_ref[y] = out


def vmem_call(kernel, out_shape, args, mib):
    return pl.pallas_call(
        kernel,
        out_shape=out_shape,
        in_specs=[pl.BlockSpec(memory_space=pltpu.VMEM)] * len(args),
        out_specs=jax.tree.map(lambda _: pl.BlockSpec(memory_space=pltpu.VMEM), out_shape),
        compiler_params=pltpu.CompilerParams(vmem_limit_bytes=min(mib, 60) * 1024 * 1024),
    )(*args)


def body(features_in, gain_outer, bias_outer, w_narrow, gain_inner, bias_inner, w_widen):
    x = features_in
    C, R, part_cols = x.shape
    n = lax.axis_size("row")
    cols = lax.axis_size("col")
    if cols > 1:
        x = lax.all_gather(x, "col", axis=2, tiled=True)
    W = x.shape[2]
    side = R * n
    halo = 24
    assert halo <= 6 * R and n % 2 == 0
    weights = prep(gain_outer, bias_outer, w_narrow, gain_inner, bias_inner, w_widen, W)

    swap = [(i, i ^ 1) for i in range(n)]
    beside = [(i, i + 1) for i in range(1, n - 1, 2)] + [(i, i - 1) for i in range(2, n, 2)]
    beyond = [(i, i + 4) for i in range(0, n - 4, 2)] + [(i, i - 4) for i in range(5, n, 2)]
    mate = lax.ppermute(x, "row", swap)
    mine = jnp.stack([x, mate])
    following = lax.ppermute(mine, "row", beside)
    sent = vmem_call(send_kernel, jax.ShapeDtypeStruct((n, 2 * R * R, 2 * C), BF), [x], mib=4 * W // 128)
    recv = lax.all_to_all(sent, "row", split_axis=0, concat_axis=0, tiled=True)
    recv, weights = lax.optimization_barrier((recv, weights))
    rows = lambda k: jax.ShapeDtypeStruct((k * R, C, W), BF)
    own, near = vmem_call(join_kernel, (rows(4), rows(2)), [recv, mine, following], mib=6 * W // 128 * W // 128)
    far = lax.ppermute(own, "row", beyond)
    near = lax.ppermute(near, "row", swap)
    other = lax.ppermute(far, "row", swap)
    out = net(own, far, near, other, *weights, R=R, side=side, halo=halo)
    if cols > 1:
        out = lax.dynamic_slice_in_dim(out, lax.axis_index("col") * part_cols, part_cols, axis=2)
    return out


def solution(mesh):
    in_specs = (P(None, ("groups", "row"), "col"), P(), P(), P(), P(), P(), P())
    out_specs = P(None, ("groups", "row"), "col")
    return jax.shard_map(body, mesh=mesh, in_specs=in_specs, out_specs=out_specs, check_vma=False)
```
